32 devices in a mesh: tag: 8 (over z, x), tile: 4 (over y, core).
Axes of the slice: x: 2, y: 2, z: 4, core: 2. Of those that a mesh axis runs over, the one named last changes fastest.
Arguments:
- species_slot: int32 [16], replicated, may hold values from 0 to 15, each once
- bulk: float32 [16, 8, 128, 128], P('tag', None, 'tile'), may hold values from 0.3 to 3
- winds: float32 [3, 8, 128, 128], P(None, None, 'tile'), may hold values from -0.35 to 0.35
- fractions: bfloat16 [2, 128, 8, 128, 128], P(None, 'tag', None, 'tile'), may hold values from 0 to 1
Outputs:
- tagged: bfloat16 [2, 128, 8, 128, 128], P(None, 'tag', None, 'tile')
The draws below stay inside these ranges and needn't reach their ends.
Inputs may be any that keep to these rules, and one draw needn't show every extreme that they name: `species_slot`: every slot appears once; slot v is held by tag group v // 2.
All inputs are finite; a program needn't handle non-finite values.
Results may differ from the reference program's by a relative error of at most 0.0035.
Values may be sent and summed in bfloat16 or wider, within the bound.
No kernel may reach another device: no remote copies, remote signals or barrier semaphores. Data moves between devices by JAX's collectives and lax.ppermute only.
A program may use at most 64 MiB of HBM per device.

```python
import math
import jax
import jax.numpy as jnp
from jax import lax

NY = 128
NZ = 8
TAG_DEV = 16
SPEC_FLIGHT = 2
SPECIES = 16
TAGS = 128
NX = 128


def block_scale(own_key, dims, split, smallest, top_value):
    level = 1.0
    for dim, blocks in split:
        heights = jax.random.uniform(jax.random.fold_in(jax.random.fold_in(own_key, 6), dim), (blocks,), jnp.float32, smallest / len(split), top_value / len(split))
        level = level * jnp.repeat(jnp.exp(heights), dims[dim] // blocks).reshape((-1,) + (1,) * (len(dims) - 1 - dim))
    return level


def setup_inputs(seed: int = 0) -> dict:
    splits = jax.random.split(jax.random.key(seed), 5)
    species_slot = jax.random.permutation(splits[0], SPECIES).astype(jnp.int32)
    bulk = jnp.clip(jnp.exp(math.log(3.0) - 2.3025851 * jax.random.uniform(splits[1], (SPECIES, NZ, NX, NY), jnp.float32) ** block_scale(splits[1], (SPECIES, NZ, NX, NY), ((0, 8), (2, 4)), -0.2, 0.2)), 0.3, 3.0)
    winds = jnp.clip(jax.random.uniform(splits[2], (3, NZ, NX, NY), jnp.float32, -0.35, 0.35) * block_scale(splits[2], (3, NZ, NX, NY), ((2, 4),), -0.4, 0.0), -0.35, 0.35)
    fractions = jnp.clip(1.0 * jax.random.uniform(splits[3], (SPEC_FLIGHT, TAGS, NZ, NX, NY), jnp.float32) ** block_scale(splits[3], (SPEC_FLIGHT, TAGS, NZ, NX, NY), ((1, 8), (3, 4)), -0.2, 0.2), 0.0, 1.0).astype(jnp.bfloat16)
    return dict(species_slot=species_slot, bulk=bulk, winds=winds, fractions=fractions)


def limited(before_two, before, after, after_two):
    centred = (7.0 * (before + after) - (before_two + after_two)) / 12.0
    return jnp.minimum(jnp.maximum(centred, jnp.minimum(before, after)), jnp.maximum(before, after))


def padded_along(values, along, lower, upper):
    widths = [(0, 0)] * values.ndim
    widths[along] = (lower, upper)
    return jnp.pad(values, widths)


def face_fluxes(cells, courant, along):
    length = cells.shape[along]
    padded = padded_along(cells, along, 2, 1)
    pieces = [lax.slice_in_dim(padded, offset, offset + length, axis=along) for offset in range(4)]
    faces = courant * limited(pieces[0], pieces[1], pieces[2], pieces[3])
    position = lax.broadcasted_iota(jnp.int32, faces.shape, along)
    return jnp.where(position == 0, 0.0, faces)


def tag_divergence(shares, faces, along):
    length = shares.shape[along]
    lower = lax.slice_in_dim(padded_along(shares, along, 1, 0), 0, length, axis=along)
    carried = jnp.maximum(faces, 0.0) * lower + jnp.minimum(faces, 0.0) * shares
    upper = padded_along(lax.slice_in_dim(carried, 1, length, axis=along), along, 0, 1)
    return upper - carried


def advect(shares, cells, flux_x, flux_y, flux_z):
    total = tag_divergence(shares, flux_x, 2) + tag_divergence(shares, flux_y, 3)
    total = total + tag_divergence(shares, flux_z, 1)
    return (shares * cells - total).astype(jnp.bfloat16)


def reference(species_slot, bulk, winds, fractions):
    results = []
    for species_index in range(SPEC_FLIGHT):
        cells = lax.dynamic_index_in_dim(bulk, species_slot[species_index], 0, keepdims=False)
        flux_x = face_fluxes(cells, winds[0], 1)
        flux_y = face_fluxes(cells, winds[1], 2)
        flux_z = face_fluxes(cells, winds[2], 0)
        blocks = fractions[species_index].reshape(TAGS // TAG_DEV, TAG_DEV, NZ, NX, NY)

        def one_block(block):
            return advect(block, cells, flux_x, flux_y, flux_z)

        moved = lax.map(one_block, blocks)
        results.append(moved.reshape(TAGS, NZ, NX, NY))
    return jnp.stack(results)
```

```python
import functools

import jax
import jax.numpy as jnp
from jax import lax
from jax.experimental import pallas as pl
from jax.experimental.pallas import tpu as pltpu
from jax.sharding import PartitionSpec as P

F32 = jnp.float32
BF16 = jnp.bfloat16
PAD = 8


def paired(value, axis, flip):
    count = lax.axis_size(axis)
    return lax.ppermute(value, axis, [(i, flip(i, count)) for i in range(count)])


def inner(i, count):
    return i ^ 1


def outer(i, count):
    return (i + 1) % count if i % 2 else (i - 1) % count


def limited(before_two, before, after, after_two):
    centred = (7.0 * (before + after) - (before_two + after_two)) / 12.0
    return jnp.minimum(jnp.maximum(centred, jnp.minimum(before, after)), jnp.maximum(before, after))


def pick_kernel(slots_ref, bulk_ref, main_ref, inner_ref, outer_ref):
    held, levels, columns, _ = bulk_ref.shape
    group = lax.axis_index("tag")
    even = lax.axis_index("tile") % 2 == 0
    for k in range(2):
        slot = slots_ref[lax.rem(group + k, 2)]
        mine = slot // held == group
        at = lax.rem(slot, held)
        main_ref[k] = jnp.where(mine, bulk_ref[at], 0.0).astype(BF16)
        for j in range(2):
            low = jnp.where(mine, bulk_ref[at, :, j, :], 0.0)
            high = jnp.where(mine, bulk_ref[at, :, columns - 2 + j, :], 0.0)
            rows = slice((2 * k + j) * levels, (2 * k + j + 1) * levels)
            inner_ref[rows, :] = jnp.where(even, high, low).astype(BF16)
            outer_ref[rows, :] = jnp.where(even, low, high).astype(BF16)


def picked(slots, bulk):
    held, levels, columns, lanes = bulk.shape
    return pl.pallas_call(
        pick_kernel,
        out_shape=(
            jax.ShapeDtypeStruct((2, levels, columns, lanes), BF16),
            jax.ShapeDtypeStruct((4 * levels, lanes), BF16),
            jax.ShapeDtypeStruct((4 * levels, lanes), BF16),
        ),
        in_specs=[
            pl.BlockSpec(memory_space=pltpu.SMEM),
            pl.BlockSpec(memory_space=pltpu.VMEM),
        ],
        out_specs=[pl.BlockSpec(memory_space=pltpu.VMEM)] * 3,
        name="pick",
    )(slots, bulk)


def advect_kernel(
    species_ref, cells_ref, rim_ref, winds_ref, above_ref, low_ref, high_ref, f_ref, _, out_ref,
    cell_ext, wind_ext, flux_ext, coef, share_ext,
):
    levels, columns, lanes = cells_ref.shape
    body = pl.ds(PAD, columns)
    first_tile = lax.axis_index("tile") == 0

    @pl.when(pl.program_id(0) == 0)
    def _():
        cell_ext[:, body, :] = cells_ref[...].astype(F32)
        rim = rim_ref[...].astype(F32)
        for j, row in enumerate((PAD - 2, PAD - 1, PAD + columns, PAD + columns + 1)):
            cell_ext[:, row, :] = rim[j * levels : (j + 1) * levels]
        wind_ext[:, 0:columns, :] = winds_ref[0]
        wind_ext[:, 0, :] = jnp.where(first_tile, 0.0, winds_ref[0, :, 0, :])
        wind_ext[:, columns, :] = above_ref[...].astype(F32)
        lane = lax.broadcasted_iota(jnp.int32, (columns, lanes), 1)
        faces = pl.ds(0, columns + 8)
        plane = [cell_ext[z, body, :] for z in range(levels)]
        zero = jnp.zeros_like(plane[0])
        at = lambda z: plane[z] if 0 <= z < levels else zero
        flux_z = [zero]
        for z in range(1, levels):
            flux_z.append(winds_ref[2, z] * limited(at(z - 2), at(z - 1), at(z), at(z + 1)))
        flux_z.append(zero)
        for z in range(levels):
            flux_ext[z, faces, :] = wind_ext[z] * limited(
                *(cell_ext[z, pl.ds(PAD - 2 + k, columns + 8), :] for k in range(4))
            )
            x_low = flux_ext[z, pl.ds(0, columns), :]
            x_up = flux_ext[z, pl.ds(1, columns), :]
            c = plane[z]
            y_two = jnp.where(lane < 2, 0.0, pltpu.roll(c, 2, 1))
            y_one = jnp.where(lane < 1, 0.0, pltpu.roll(c, 1, 1))
            y_next = jnp.where(lane == lanes - 1, 0.0, pltpu.roll(c, lanes - 1, 1))
            y_low = winds_ref[1, z] * limited(y_two, y_one, c, y_next)
            y_low = jnp.where(lane < 1, 0.0, y_low)
            y_up = pltpu.roll(y_low, lanes - 1, 1)
            centre = c
            for d, (low, up) in enumerate(((x_low, x_up), (y_low, y_up), (flux_z[z], flux_z[z + 1]))):
                inward = jnp.minimum(low, 0.0)
                outward = jnp.maximum(up, 0.0)
                coef[2 * d, z] = low - inward
                coef[2 * d + 1, z] = outward - up
                centre = centre + (inward - outward)
            coef[6, z] = centre

    def one_tag(i, carry):
        share_ext[:, PAD - 1, :] = low_ref[i].astype(F32)
        share_ext[:, PAD + columns, :] = high_ref[i].astype(F32)
        plane = [f_ref[i, z].astype(F32) for z in range(levels)]
        for z in range(levels):
            share_ext[z, body, :] = plane[z]
        for z in range(levels):
            f = plane[z]
            total = coef[6, z] * f
            total += coef[0, z] * share_ext[z, pl.ds(PAD - 1, columns), :]
            total += coef[1, z] * share_ext[z, pl.ds(PAD + 1, columns), :]
            total += coef[2, z] * pltpu.roll(f, 1, 1)
            total += coef[3, z] * pltpu.roll(f, lanes - 1, 1)
            if z > 0:
                total += coef[4, z] * plane[z - 1]
            if z < levels - 1:
                total += coef[5, z] * plane[z + 1]
            out_ref[i, z] = total.astype(out_ref.dtype)
        return carry

    lax.fori_loop(0, f_ref.shape[0], one_tag, 0)


def advected(which, cells, rim, winds, above, low, high, fractions, out, step):
    species, tags, levels, columns, lanes = fractions.shape
    whole = pl.BlockSpec(memory_space=pltpu.VMEM)
    halo = pl.BlockSpec((None, step, levels, lanes), lambda i, s: (s[0], i, 0, 0))
    block = pl.BlockSpec((None, step, levels, columns, lanes), lambda i, s: (s[0], i, 0, 0, 0))
    alias = {8: 0} if out is not None else {}
    if out is None:
        out = jnp.zeros((8, 128), BF16)
    return pl.pallas_call(
        advect_kernel,
        out_shape=jax.ShapeDtypeStruct(fractions.shape, fractions.dtype),
        grid_spec=pltpu.PrefetchScalarGridSpec(
            num_scalar_prefetch=1,
            grid=(tags // step,),
            in_specs=[whole, whole, whole, whole, halo, halo, block, pl.BlockSpec(memory_space=pl.ANY)],
            out_specs=block,
            scratch_shapes=[
                pltpu.VMEM((levels, columns + 24, lanes), F32),
                pltpu.VMEM((levels, columns + 8, lanes), F32),
                pltpu.VMEM((levels, columns + 8, lanes), F32),
                pltpu.VMEM((7, levels, columns, lanes), F32),
                pltpu.VMEM((levels, columns + 16, lanes), F32),
            ],
        ),
        input_output_aliases=alias,
        name="advect",
    )(which, cells, rim, winds, above, low, high, fractions, out)


def shards(species_slot, bulk, winds, fractions):
    held, levels, columns, lanes = bulk.shape
    species, tags = fractions.shape[:2]
    group, tile = lax.axis_index("tag"), lax.axis_index("tile")
    groups, tiles = lax.axis_size("tag"), lax.axis_size("tile")
    even = tile % 2 == 0

    main, inner_edge, outer_edge = picked(species_slot, bulk)
    from_inner = paired(inner_edge, "tile", inner)
    from_outer = paired(outer_edge, "tile", outer)
    low = jnp.where(even, from_outer, from_inner).reshape(2, 2 * levels, lanes)
    high = jnp.where(even, from_inner, from_outer).reshape(2, 2 * levels, lanes)
    low = jnp.where(tile == 0, jnp.zeros_like(low), low)
    high = jnp.where(tile == tiles - 1, jnp.zeros_like(high), high)
    rows = jnp.concatenate([main.reshape(2, levels * columns, lanes), low, high], axis=1)

    own = rows[0] + paired(rows[1], "tag", inner)
    bit = 2
    while bit < groups:
        own = own + paired(own, "tag", lambda i, count: i ^ bit)
        bit *= 2
    other = paired(own, "tag", inner)

    first, last = fractions[:, :, :, 0, :], fractions[:, :, :, columns - 1, :]
    top = winds[0, :, 0, :].astype(BF16)
    size = species * tags * levels
    inner_rows = jnp.concatenate([jnp.where(even, last, first).reshape(size, lanes), top])
    outer_rows = jnp.concatenate([jnp.where(even, first, last).reshape(size, lanes), top])
    got_inner = paired(inner_rows, "tile", inner)
    got_outer = paired(outer_rows, "tile", outer)
    below = jnp.where(even, got_outer, got_inner)
    beyond = jnp.where(even, got_inner, got_outer)
    below = jnp.where(tile == 0, jnp.zeros_like(below), below)
    beyond = jnp.where(tile == tiles - 1, jnp.zeros_like(beyond), beyond)
    share_low = below[:size].reshape(species, tags, levels, lanes)
    share_high = beyond[:size].reshape(species, tags, levels, lanes)
    above = beyond[size:]

    step = 4
    out = None
    for k, cells in enumerate((own, other)):
        which = (lax.rem(group + k, 2))[None]
        out = advected(
            which, cells[: levels * columns].reshape(levels, columns, lanes), cells[levels * columns :],
            winds, above, share_low, share_high, fractions, out, step,
        )
    return out


def solution(mesh):
    placed = (
        P(),
        P("tag", None, "tile", None),
        P(None, None, "tile", None),
        P(None, "tag", None, "tile", None),
    )
    return jax.shard_map(
        shards,
        mesh=mesh,
        in_specs=placed,
        out_specs=P(None, "tag", None, "tile", None),
        check_vma=False,
    )
```

```python
import jax
import jax.numpy as jnp
from jax import lax
from jax.experimental import pallas as pl
from jax.experimental.pallas import tpu as pltpu
from jax.sharding import PartitionSpec as P


F32 = jnp.float32
BF16 = jnp.bfloat16
I16 = jnp.int16
PAD = 8
SCALE = 10240.0
TOGETHER = 4
LIMIT = pltpu.CompilerParams(vmem_limit_bytes=16 * 2**20)


def in_vmem(value):
    return pltpu.with_memory_space_constraint(value, pltpu.VMEM)


def in_hbm(value):
    return pltpu.with_memory_space_constraint(value, pltpu.HBM)


def paired(value, axis, flip):
    count = lax.axis_size(axis)
    return lax.ppermute(value, axis, [(i, flip(i, count)) for i in range(count)])


def inner(i, count):
    return i ^ 1


def outer(i, count):
    return (i + 1) % count if i % 2 else (i - 1) % count


def limited(before_two, before, after, after_two):
    centred = (7.0 * (before + after) - (before_two + after_two)) / 12.0
    return jnp.minimum(jnp.maximum(centred, jnp.minimum(before, after)), jnp.maximum(before, after))


def coded(values):
    return (values * SCALE + 0.5).astype(jnp.int32).astype(I16)


def decoded(codes):
    return codes.astype(jnp.int32).astype(F32) * (1.0 / SCALE)


def pick_kernel(slots_hbm, bulk_hbm, main_ref, inner_ref, outer_ref, slots_ref, bulk_ref, sems):
    held, levels, columns, _ = bulk_ref.shape
    table = pltpu.make_async_copy(slots_hbm, slots_ref, sems.at[0])
    field = pltpu.make_async_copy(bulk_hbm, bulk_ref, sems.at[1])
    table.start()
    field.start()
    group = lax.axis_index("tag")
    even = lax.axis_index("tile") % 2 == 0
    table.wait()
    field.wait()
    for k in range(2):
        slot = slots_ref[lax.rem(group + k, 2)]
        mine = slot // held == group
        at = lax.rem(slot, held)
        scale = jnp.where(mine, 1.0, 0.0)
        for z in range(levels):
            main_ref[k, pl.ds(z * columns, columns), :] = coded(bulk_ref[at, z] * scale)
        for j in range(2):
            low = bulk_ref[at, :, j, :]
            high = bulk_ref[at, :, columns - 2 + j, :]
            rows = pl.ds((2 * k + j) * levels, levels)
            inner_ref[rows, :] = coded(jnp.where(even, high, low) * scale)
            outer_ref[rows, :] = coded(jnp.where(even, low, high) * scale)


def picked(slots, bulk):
    _, levels, columns, lanes = bulk.shape
    whole = pl.BlockSpec(memory_space=pltpu.VMEM)
    far = pl.BlockSpec(memory_space=pltpu.HBM)
    edge = jax.ShapeDtypeStruct((4 * levels, lanes), I16)
    return pl.pallas_call(
        pick_kernel,
        out_shape=(jax.ShapeDtypeStruct((2, levels * columns, lanes), I16), edge, edge),
        in_specs=[far, far],
        out_specs=[whole] * 3,
        scratch_shapes=[
            pltpu.SMEM(slots.shape, slots.dtype),
            pltpu.VMEM(bulk.shape, bulk.dtype),
            pltpu.SemaphoreType.DMA((2,)),
        ],
        compiler_params=LIMIT,
        name="pick",
    )(in_hbm(slots), in_hbm(bulk))


def stage_kernel(f_hbm, winds_hbm, f_ref, winds_ref, inner_ref, outer_ref, sems):
    species, tags, levels, columns, _ = f_ref.shape
    even = lax.axis_index("tile") % 2 == 0
    parts = [(k, j) for k in range(species) for j in range(tags // TOGETHER)]
    copies = [pltpu.make_async_copy(winds_hbm, winds_ref, sems.at[len(parts)])]
    for n, (k, j) in enumerate(parts):
        part = pl.ds(j * TOGETHER, TOGETHER)
        copies.append(pltpu.make_async_copy(f_hbm.at[k, part], f_ref.at[k, part], sems.at[n]))
    for copy in copies:
        copy.start()
    copies[0].wait()
    rows = pl.ds(species * tags * levels, levels)
    top = winds_ref[0, :, 0, :].astype(BF16)
    inner_ref[rows, :] = top
    outer_ref[rows, :] = top
    for n, (k, j) in enumerate(parts):
        copies[n + 1].wait()
        for t in range(j * TOGETHER, (j + 1) * TOGETHER):
            first = f_ref[k, t, :, 0, :].astype(F32)
            last = f_ref[k, t, :, columns - 1, :].astype(F32)
            rows = pl.ds((k * tags + t) * levels, levels)
            inner_ref[rows, :] = jnp.where(even, last, first).astype(BF16)
            outer_ref[rows, :] = jnp.where(even, first, last).astype(BF16)


def staged(fractions, winds):
    species, tags, levels, _, lanes = fractions.shape
    whole = pl.BlockSpec(memory_space=pltpu.VMEM)
    far = pl.BlockSpec(memory_space=pltpu.HBM)
    rows = jax.ShapeDtypeStruct(((species * tags + 1) * levels, lanes), BF16)
    return pl.pallas_call(
        stage_kernel,
        out_shape=(
            jax.ShapeDtypeStruct(fractions.shape, fractions.dtype),
            jax.ShapeDtypeStruct(winds.shape, winds.dtype),
            rows,
            rows,
        ),
        in_specs=[far, far],
        out_specs=[whole] * 4,
        scratch_shapes=[pltpu.SemaphoreType.DMA((species * (tags // TOGETHER) + 1,))],
        compiler_params=LIMIT,
        name="stage",
    )(in_hbm(fractions), in_hbm(winds))


def advect_kernel(
    species_ref, cells_ref, winds_ref, inner_ref, outer_ref, f_ref, _, out_ref,
    cell_ext, wind_ext, flux_ext, coef, share_ext, result, sems,
):
    species, tags, levels, columns, lanes = f_ref.shape
    own = species_ref[0]
    body = pl.ds(PAD, columns)
    tile = lax.axis_index("tile")
    even = tile % 2 == 0
    last_tile = tile == lax.axis_size("tile") - 1

    def below(rows):
        return jnp.where(even, outer_ref[rows, :].astype(F32), inner_ref[rows, :].astype(F32))

    def beyond(rows):
        return jnp.where(even, inner_ref[rows, :].astype(F32), outer_ref[rows, :].astype(F32))

    for z in range(levels):
        cell_ext[z, body, :] = decoded(cells_ref[pl.ds(z * columns, columns), :])
    for j, row in enumerate((PAD - 2, PAD - 1, PAD + columns, PAD + columns + 1)):
        cell_ext[:, row, :] = decoded(cells_ref[pl.ds((columns + j) * levels, levels), :])
    wind_ext[:, 0:columns, :] = winds_ref[0]
    wind_ext[:, 0, :] = jnp.where(tile == 0, 0.0, winds_ref[0, :, 0, :])
    above = beyond(pl.ds(species * tags * levels, levels))
    wind_ext[:, columns, :] = jnp.where(last_tile, 0.0, above)
    lane = lax.broadcasted_iota(jnp.int32, (columns, lanes), 1)
    faces = pl.ds(0, columns + 8)
    plane = [cell_ext[z, body, :] for z in range(levels)]
    zero = jnp.zeros_like(plane[0])
    at = lambda z: plane[z] if 0 <= z < levels else zero
    flux_z = [zero]
    for z in range(1, levels):
        flux_z.append(winds_ref[2, z] * limited(at(z - 2), at(z - 1), at(z), at(z + 1)))
    flux_z.append(zero)
    for z in range(levels):
        flux_ext[z, faces, :] = wind_ext[z] * limited(
            *(cell_ext[z, pl.ds(PAD - 2 + k, columns + 8), :] for k in range(4))
        )
        x_low = flux_ext[z, pl.ds(0, columns), :]
        x_up = flux_ext[z, pl.ds(1, columns), :]
        c = plane[z]
        y_two = jnp.where(lane < 2, 0.0, pltpu.roll(c, 2, 1))
        y_one = jnp.where(lane < 1, 0.0, pltpu.roll(c, 1, 1))
        y_next = jnp.where(lane == lanes - 1, 0.0, pltpu.roll(c, lanes - 1, 1))
        y_low = winds_ref[1, z] * limited(y_two, y_one, c, y_next)
        y_low = jnp.where(lane < 1, 0.0, y_low)
        y_up = pltpu.roll(y_low, lanes - 1, 1)
        centre = c
        for d, (low, up) in enumerate(((x_low, x_up), (y_low, y_up), (flux_z[z], flux_z[z + 1]))):
            inward = jnp.minimum(low, 0.0)
            outward = jnp.maximum(up, 0.0)
            coef[2 * d, z] = low - inward
            coef[2 * d + 1, z] = outward - up
            centre = centre + (inward - outward)
        coef[6, z] = centre

    def some_tags(base, carry):
        planes = []
        for p in range(TOGETHER):
            i = base * TOGETHER + p
            rows = pl.ds((own * tags + i) * levels, levels)
            share_ext[p, :, PAD - 1, :] = below(rows)
            share_ext[p, :, PAD + columns, :] = beyond(rows)
            plane = [f_ref[own, i, z].astype(F32) for z in range(levels)]
            for z in range(levels):
                share_ext[p, z, body, :] = plane[z]
            planes.append(plane)
        for z in range(levels):
            cs = [coef[k, z] for k in range(7)]
            for p, plane in enumerate(planes):
                f = plane[z]
                total = cs[6] * f
                total += cs[0] * share_ext[p, z, pl.ds(PAD - 1, columns), :]
                total += cs[1] * share_ext[p, z, pl.ds(PAD + 1, columns), :]
                total += cs[2] * pltpu.roll(f, 1, 1)
                total += cs[3] * pltpu.roll(f, lanes - 1, 1)
                if z > 0:
                    total += cs[4] * plane[z - 1]
                if z < levels - 1:
                    total += cs[5] * plane[z + 1]
                result[base * TOGETHER + p, z] = total.astype(out_ref.dtype)
        return carry

    def stored(j):
        part = pl.ds(j * TOGETHER, TOGETHER)
        return pltpu.make_async_copy(result.at[part], out_ref.at[own, part], sems.at[j])

    for j in range(tags // TOGETHER):
        lax.fori_loop(j, j + 1, some_tags, 0)
        stored(j).start()
    for j in range(tags // TOGETHER):
        stored(j).wait()


def advected(which, cells, winds, from_inner, from_outer, fractions, out):
    _, tags, levels, columns, lanes = fractions.shape
    whole = pl.BlockSpec(memory_space=pltpu.VMEM)
    scalar = pl.BlockSpec(memory_space=pltpu.SMEM)
    place = pl.BlockSpec(memory_space=pl.ANY)
    first = out is None
    return pl.pallas_call(
        advect_kernel,
        out_shape=jax.ShapeDtypeStruct(fractions.shape, fractions.dtype),
        in_specs=[scalar, whole, whole, whole, whole, whole, scalar if first else place],
        out_specs=place,
        scratch_shapes=[
            pltpu.VMEM((levels, columns + 24, lanes), F32),
            pltpu.VMEM((levels, columns + 8, lanes), F32),
            pltpu.VMEM((levels, columns + 8, lanes), F32),
            pltpu.VMEM((7, levels, columns, lanes), F32),
            pltpu.VMEM((TOGETHER, levels, columns + 16, lanes), F32),
            pltpu.VMEM((tags, levels, columns, lanes), fractions.dtype),
            pltpu.SemaphoreType.DMA((tags // TOGETHER,)),
        ],
        input_output_aliases={} if first else {6: 0},
        compiler_params=LIMIT,
        name="advect",
    )(which, in_vmem(cells), winds, in_vmem(from_inner), in_vmem(from_outer), fractions, which if first else out)


def shards(species_slot, bulk, winds, fractions):
    _, levels, _, lanes = bulk.shape
    group, tile = lax.axis_index("tag"), lax.axis_index("tile")
    groups, tiles = lax.axis_size("tag"), lax.axis_size("tile")
    even = tile % 2 == 0

    main, inner_edge, outer_edge = picked(species_slot, bulk)
    from_outer = paired(outer_edge, "tile", outer)
    from_inner = paired(inner_edge, "tile", inner)
    low = jnp.where(even, from_outer, from_inner).reshape(2, 2 * levels, lanes)
    high = jnp.where(even, from_inner, from_outer).reshape(2, 2 * levels, lanes)
    low = jnp.where(tile == 0, jnp.zeros_like(low), low)
    high = jnp.where(tile == tiles - 1, jnp.zeros_like(high), high)
    rows = jnp.concatenate([main, low, high], axis=1)

    fractions, winds, inner_rows, outer_rows = staged(fractions, winds)
    got_inner = paired(inner_rows, "tile", inner)
    got_outer = paired(outer_rows, "tile", outer)

    crossed = paired(rows[1], "tag", inner)
    own = rows[0] + crossed
    bit = 2
    while bit < groups:
        came = paired(own, "tag", lambda i, count: i ^ bit)
        own = own + came
        bit *= 2
    other = paired(own, "tag", inner)

    out = None
    for k, cells in enumerate((own, other)):
        which = lax.rem(group + k, 2)[None]
        out = advected(which, cells, winds, got_inner, got_outer, fractions, out)
    return out


def solution(mesh):
    placed = (
        P(),
        P("tag", None, "tile", None),
        P(None, None, "tile", None),
        P(None, "tag", None, "tile", None),
    )
    return jax.shard_map(
        shards,
        mesh=mesh,
        in_specs=placed,
        out_specs=P(None, "tag", None, "tile", None),
        check_vma=False,
    )
```

```python
import functools

import jax
import jax.numpy as jnp
from jax import lax
from jax.experimental import pallas as pl
from jax.experimental.pallas import tpu as pltpu
from jax.sharding import PartitionSpec as P


F32 = jnp.float32
BF16 = jnp.bfloat16
I16 = jnp.int16
PAD = 8
SCALE = 10240.0
TOGETHER = 4
LIMIT = pltpu.CompilerParams(vmem_limit_bytes=16 * 2**20)


def in_vmem(value):
    return pltpu.with_memory_space_constraint(value, pltpu.VMEM)


def in_hbm(value):
    return pltpu.with_memory_space_constraint(value, pltpu.HBM)


def paired(value, axis, flip):
    count = lax.axis_size(axis)
    return lax.ppermute(value, axis, [(i, flip(i, count)) for i in range(count)])


def inner(i, count):
    return i ^ 1


def outer(i, count):
    return (i + 1) % count if i % 2 else (i - 1) % count


def limited(before_two, before, after, after_two):
    centred = (7.0 * (before + after) - (before_two + after_two)) / 12.0
    return jnp.minimum(jnp.maximum(centred, jnp.minimum(before, after)), jnp.maximum(before, after))


def coded(values, scale):
    return (values * scale + 0.5).astype(jnp.int32).astype(I16)


def decoded(codes):
    return codes.astype(jnp.int32).astype(F32) * (1.0 / SCALE)


def pick_kernel(slots_hbm, bulk_hbm, main_ref, inner_ref, outer_ref, slots_ref, bulk_ref, sems):
    held, levels, columns, _ = bulk_ref.shape
    table = pltpu.make_async_copy(slots_hbm, slots_ref, sems.at[0])
    field = pltpu.make_async_copy(bulk_hbm, bulk_ref, sems.at[1])
    table.start()
    field.start()
    group = lax.axis_index("tag")
    even = lax.axis_index("tile") % 2 == 0
    table.wait()
    field.wait()
    for k in range(2):
        slot = slots_ref[lax.rem(group + k, 2)]
        at = lax.rem(slot, held)
        scale = jnp.where(slot // held == group, SCALE, 0.0)
        for z in range(levels):
            main_ref[k, pl.ds(z * columns, columns), :] = coded(bulk_ref[at, z], scale)
        for j in range(2):
            low = bulk_ref[at, :, j, :]
            high = bulk_ref[at, :, columns - 2 + j, :]
            rows = pl.ds((2 * k + j) * levels, levels)
            inner_ref[rows, :] = coded(jnp.where(even, high, low), scale)
            outer_ref[rows, :] = coded(jnp.where(even, low, high), scale)


def picked(slots, bulk):
    _, levels, columns, lanes = bulk.shape
    whole = pl.BlockSpec(memory_space=pltpu.VMEM)
    far = pl.BlockSpec(memory_space=pltpu.HBM)
    edge = jax.ShapeDtypeStruct((4 * levels, lanes), I16)
    return pl.pallas_call(
        pick_kernel,
        out_shape=(jax.ShapeDtypeStruct((2, levels * columns, lanes), I16), edge, edge),
        in_specs=[far, far],
        out_specs=[whole] * 3,
        scratch_shapes=[
            pltpu.SMEM(slots.shape, slots.dtype),
            pltpu.VMEM(bulk.shape, bulk.dtype),
            pltpu.SemaphoreType.DMA((2,)),
        ],
        compiler_params=LIMIT,
        name="pick",
    )(in_hbm(slots), in_hbm(bulk))


def stage_kernel(f_hbm, winds_hbm, f_ref, winds_ref, inner_ref, outer_ref, sems):
    species, tags, levels, columns, _ = f_ref.shape
    even = lax.axis_index("tile") % 2 == 0
    parts = [(k, j) for k in range(species) for j in range(tags // TOGETHER)]
    copies = [pltpu.make_async_copy(winds_hbm, winds_ref, sems.at[len(parts)])]
    for n, (k, j) in enumerate(parts):
        part = pl.ds(j * TOGETHER, TOGETHER)
        copies.append(pltpu.make_async_copy(f_hbm.at[k, part], f_ref.at[k, part], sems.at[n]))
    for copy in copies:
        copy.start()
    copies[0].wait()
    rows = pl.ds(species * tags * levels, levels)
    top = winds_ref[0, :, 0, :].astype(BF16)
    inner_ref[rows, :] = top
    outer_ref[rows, :] = top
    for n, (k, j) in enumerate(parts):
        copies[n + 1].wait()
        for t in range(j * TOGETHER, (j + 1) * TOGETHER):
            first = f_ref[k, t, :, 0, :].astype(F32)
            last = f_ref[k, t, :, columns - 1, :].astype(F32)
            rows = pl.ds((k * tags + t) * levels, levels)
            inner_ref[rows, :] = jnp.where(even, last, first).astype(BF16)
            outer_ref[rows, :] = jnp.where(even, first, last).astype(BF16)


def staged(fractions, winds):
    species, tags, levels, _, lanes = fractions.shape
    whole = pl.BlockSpec(memory_space=pltpu.VMEM)
    far = pl.BlockSpec(memory_space=pltpu.HBM)
    rows = jax.ShapeDtypeStruct(((species * tags + 1) * levels, lanes), BF16)
    return pl.pallas_call(
        stage_kernel,
        out_shape=(
            jax.ShapeDtypeStruct(fractions.shape, fractions.dtype),
            jax.ShapeDtypeStruct(winds.shape, winds.dtype),
            rows,
            rows,
        ),
        in_specs=[far, far],
        out_specs=[whole] * 4,
        scratch_shapes=[pltpu.SemaphoreType.DMA((species * (tags // TOGETHER) + 1,))],
        compiler_params=LIMIT,
        name="stage",
    )(in_hbm(fractions), in_hbm(winds))


def advect_kernel(
    last, species_ref, cells_ref, rims_ref, met_ref, winds_ref, inner_ref, outer_ref, f_ref, *refs
):
    if last:
        before, out_ref, cell_ext, wind_ext, flux_ext, coef, share_ext, result, sems = refs
    else:
        result, cell_ext, wind_ext, flux_ext, coef, share_ext = refs
    species, tags, levels, columns, lanes = f_ref.shape
    own = species_ref[0]
    body = pl.ds(PAD, columns)
    if last:
        earlier = pltpu.make_async_copy(before, out_ref.at[1 - own], sems.at[tags // TOGETHER])
        earlier.start()
    tile = lax.axis_index("tile")
    even = tile % 2 == 0
    last_tile = tile == lax.axis_size("tile") - 1

    def below(rows):
        return jnp.where(even, outer_ref[rows, :].astype(F32), inner_ref[rows, :].astype(F32))

    def beyond(rows):
        return jnp.where(even, inner_ref[rows, :].astype(F32), outer_ref[rows, :].astype(F32))

    for z in range(levels):
        cell_ext[z, body, :] = decoded(cells_ref[pl.ds(z * columns, columns), :])
    start = rims_ref.shape[0] - 8 * levels

    def rim(row):
        mine = pl.ds(start + (row + 2 * last) * levels, levels)
        theirs = pl.ds((row + 2 - 2 * last) * levels, levels)
        return decoded(rims_ref[mine, :]) + decoded(met_ref[theirs, :])

    for j in range(2):
        from_inner, from_outer = rim(j), rim(4 + j)
        low = jnp.where(even, from_outer, from_inner)
        high = jnp.where(even, from_inner, from_outer)
        cell_ext[:, PAD - 2 + j, :] = jnp.where(tile == 0, 0.0, low)
        cell_ext[:, PAD + columns + j, :] = jnp.where(last_tile, 0.0, high)
    wind_ext[:, 0:columns, :] = winds_ref[0]
    wind_ext[:, 0, :] = jnp.where(tile == 0, 0.0, winds_ref[0, :, 0, :])
    above = beyond(pl.ds(species * tags * levels, levels))
    wind_ext[:, columns, :] = jnp.where(last_tile, 0.0, above)
    lane = lax.broadcasted_iota(jnp.int32, (columns, lanes), 1)
    faces = pl.ds(0, columns + 8)
    plane = [cell_ext[z, body, :] for z in range(levels)]
    zero = jnp.zeros_like(plane[0])
    at = lambda z: plane[z] if 0 <= z < levels else zero
    flux_z = [zero]
    for z in range(1, levels):
        flux_z.append(winds_ref[2, z] * limited(at(z - 2), at(z - 1), at(z), at(z + 1)))
    flux_z.append(zero)
    for z in range(levels):
        flux_ext[z, faces, :] = wind_ext[z] * limited(
            *(cell_ext[z, pl.ds(PAD - 2 + k, columns + 8), :] for k in range(4))
        )
        x_low = flux_ext[z, pl.ds(0, columns), :]
        x_up = flux_ext[z, pl.ds(1, columns), :]
        c = plane[z]
        y_two = jnp.where(lane < 2, 0.0, pltpu.roll(c, 2, 1))
        y_one = jnp.where(lane < 1, 0.0, pltpu.roll(c, 1, 1))
        y_next = jnp.where(lane == lanes - 1, 0.0, pltpu.roll(c, lanes - 1, 1))
        y_low = winds_ref[1, z] * limited(y_two, y_one, c, y_next)
        y_low = jnp.where(lane < 1, 0.0, y_low)
        y_up = pltpu.roll(y_low, lanes - 1, 1)
        centre = c
        for d, (low, up) in enumerate(((x_low, x_up), (y_low, y_up), (flux_z[z], flux_z[z + 1]))):
            inward = jnp.minimum(low, 0.0)
            outward = jnp.maximum(up, 0.0)
            coef[2 * d, z] = low - inward
            coef[2 * d + 1, z] = outward - up
            centre = centre + (inward - outward)
        coef[6, z] = centre

    def some_tags(base, carry):
        planes = []
        for p in range(TOGETHER):
            i = base * TOGETHER + p
            rows = pl.ds((own * tags + i) * levels, levels)
            share_ext[p, :, PAD - 1, :] = below(rows)
            share_ext[p, :, PAD + columns, :] = beyond(rows)
            plane = [f_ref[own, i, z].astype(F32) for z in range(levels)]
            for z in range(levels):
                share_ext[p, z, body, :] = plane[z]
            planes.append(plane)
        for z in range(levels):
            cs = [coef[k, z] for k in range(7)]
            for p, plane in enumerate(planes):
                f = plane[z]
                total = cs[6] * f
                total += cs[0] * share_ext[p, z, pl.ds(PAD - 1, columns), :]
                total += cs[1] * share_ext[p, z, pl.ds(PAD + 1, columns), :]
                total += cs[2] * pltpu.roll(f, 1, 1)
                total += cs[3] * pltpu.roll(f, lanes - 1, 1)
                if z > 0:
                    total += cs[4] * plane[z - 1]
                if z < levels - 1:
                    total += cs[5] * plane[z + 1]
                result[base * TOGETHER + p, z] = total.astype(result.dtype)
        return carry

    def stored(j):
        part = pl.ds(j * TOGETHER, TOGETHER)
        return pltpu.make_async_copy(result.at[part], out_ref.at[own, part], sems.at[j])

    for j in range(tags // TOGETHER):
        lax.fori_loop(j, j + 1, some_tags, 0)
        if last:
            stored(j).start()
    if last:
        earlier.wait()
        for j in range(tags // TOGETHER):
            stored(j).wait()


def advected(which, cells, rims, met, winds, from_inner, from_outer, fractions, before):
    _, tags, levels, columns, lanes = fractions.shape
    last = before is not None
    whole = pl.BlockSpec(memory_space=pltpu.VMEM)
    scalar = pl.BlockSpec(memory_space=pltpu.SMEM)
    one = (tags, levels, columns, lanes)
    scratch = [
        pltpu.VMEM((levels, columns + 24, lanes), F32),
        pltpu.VMEM((levels, columns + 8, lanes), F32),
        pltpu.VMEM((levels, columns + 8, lanes), F32),
        pltpu.VMEM((7, levels, columns, lanes), F32),
        pltpu.VMEM((TOGETHER, levels, columns + 16, lanes), F32),
    ]
    operands = [which, in_vmem(cells), in_vmem(rims), in_vmem(met), winds, in_vmem(from_inner), in_vmem(from_outer), fractions]
    if last:
        scratch += [pltpu.VMEM(one, fractions.dtype), pltpu.SemaphoreType.DMA((tags // TOGETHER + 1,))]
        operands.append(in_vmem(before))
    return pl.pallas_call(
        functools.partial(advect_kernel, last),
        out_shape=jax.ShapeDtypeStruct(fractions.shape if last else one, fractions.dtype),
        in_specs=[scalar] + [whole] * (len(operands) - 1),
        out_specs=pl.BlockSpec(memory_space=pl.ANY) if last else whole,
        scratch_shapes=scratch,
        compiler_params=LIMIT,
        name="advect",
    )(*operands)


def shards(species_slot, bulk, winds, fractions):
    _, levels, columns, _ = bulk.shape
    group, groups = lax.axis_index("tag"), lax.axis_size("tag")
    size = levels * columns

    main, inner_edge, outer_edge = picked(species_slot, bulk)
    came = paired(main[1], "tag", inner)
    rim_outer = paired(outer_edge, "tile", outer)
    rim_inner = paired(inner_edge, "tile", inner)
    fractions, winds, inner_rows, outer_rows = staged(fractions, winds)
    own = jnp.concatenate([main[0] + came, rim_inner, rim_outer])
    bit = 2
    while bit < groups:
        came = paired(own, "tag", lambda i, count: i ^ bit)
        own = own + came
        bit *= 2
    got_inner = paired(inner_rows, "tile", inner)
    got_outer = paired(outer_rows, "tile", outer)
    met = paired(own[size:], "tag", inner)
    other = paired(own[:size], "tag", inner)

    which = lax.rem(group, 2)[None]
    done = advected(which, own, own, met, winds, got_inner, got_outer, fractions, None)
    return advected(1 - which, other, own, met, winds, got_inner, got_outer, fractions, done)


def solution(mesh):
    placed = (
        P(),
        P("tag", None, "tile", None),
        P(None, None, "tile", None),
        P(None, "tag", None, "tile", None),
    )
    return jax.shard_map(
        shards,
        mesh=mesh,
        in_specs=placed,
        out_specs=P(None, "tag", None, "tile", None),
        check_vma=False,
    )
```

```python
import jax
import jax.numpy as jnp
from jax import lax
from jax.experimental import pallas as pl
from jax.experimental.pallas import tpu as pltpu
from jax.sharding import PartitionSpec as P


F32 = jnp.float32
BF16 = jnp.bfloat16
I16 = jnp.int16
PAD = 8
SCALE = 10240.0
TOGETHER = 8
LIMIT = pltpu.CompilerParams(vmem_limit_bytes=16 * 2**20)


def in_vmem(value):
    return pltpu.with_memory_space_constraint(value, pltpu.VMEM)


def in_hbm(value):
    return pltpu.with_memory_space_constraint(value, pltpu.HBM)


def paired(value, axis, flip):
    count = lax.axis_size(axis)
    return lax.ppermute(value, axis, [(i, flip(i, count)) for i in range(count)])


def inner(i, count):
    return i ^ 1


def outer(i, count):
    return (i + 1) % count if i % 2 else (i - 1) % count


def limited(before_two, before, after, after_two):
    centred = (7.0 * (before + after) - (before_two + after_two)) / 12.0
    return jnp.minimum(jnp.maximum(centred, jnp.minimum(before, after)), jnp.maximum(before, after))


def coded(values, scale):
    return (values * scale + 0.5).astype(jnp.int32).astype(I16)


def decoded(codes):
    return codes.astype(jnp.int32).astype(F32) * (1.0 / SCALE)


def pick_kernel(slots_hbm, bulk_hbm, main_ref, inner_ref, outer_ref, slots_ref, bulk_ref, sems):
    held, levels, columns, _ = bulk_ref.shape
    table = pltpu.make_async_copy(slots_hbm, slots_ref, sems.at[0])
    field = pltpu.make_async_copy(bulk_hbm, bulk_ref, sems.at[1])
    table.start()
    field.start()
    group = lax.axis_index("tag")
    even = lax.axis_index("tile") % 2 == 0
    table.wait()
    field.wait()
    for k in range(2):
        slot = slots_ref[lax.rem(group + k, 2)]
        at = lax.rem(slot, held)
        scale = jnp.where(slot // held == group, SCALE, 0.0)
        for z in range(levels):
            main_ref[k, pl.ds(z * columns, columns), :] = coded(bulk_ref[at, z], scale)
        for j in range(2):
            low = bulk_ref[at, :, j, :]
            high = bulk_ref[at, :, columns - 2 + j, :]
            rows = pl.ds((2 * k + j) * levels, levels)
            inner_ref[rows, :] = coded(jnp.where(even, high, low), scale)
            outer_ref[rows, :] = coded(jnp.where(even, low, high), scale)


def picked(slots, bulk):
    _, levels, columns, lanes = bulk.shape
    whole = pl.BlockSpec(memory_space=pltpu.VMEM)
    far = pl.BlockSpec(memory_space=pltpu.HBM)
    edge = jax.ShapeDtypeStruct((4 * levels, lanes), I16)
    return pl.pallas_call(
        pick_kernel,
        out_shape=(jax.ShapeDtypeStruct((2, levels * columns, lanes), I16), edge, edge),
        in_specs=[far, far],
        out_specs=[whole] * 3,
        scratch_shapes=[
            pltpu.SMEM(slots.shape, slots.dtype),
            pltpu.VMEM(bulk.shape, bulk.dtype),
            pltpu.SemaphoreType.DMA((2,)),
        ],
        compiler_params=LIMIT,
        name="pick",
    )(in_hbm(slots), in_hbm(bulk))


def stage_kernel(f_hbm, winds_hbm, f_ref, winds_ref, inner_ref, outer_ref, sems):
    species, tags, levels, columns, _ = f_ref.shape
    even = lax.axis_index("tile") % 2 == 0
    parts = [(k, j) for k in range(species) for j in range(tags // TOGETHER)]
    copies = [pltpu.make_async_copy(winds_hbm, winds_ref, sems.at[len(parts)])]
    for n, (k, j) in enumerate(parts):
        part = pl.ds(j * TOGETHER, TOGETHER)
        copies.append(pltpu.make_async_copy(f_hbm.at[k, part], f_ref.at[k, part], sems.at[n]))
    for copy in copies:
        copy.start()
    copies[0].wait()
    rows = pl.ds(species * tags * levels, levels)
    top = winds_ref[0, :, 0, :].astype(BF16)
    inner_ref[rows, :] = top
    outer_ref[rows, :] = top
    for n, (k, j) in enumerate(parts):
        copies[n + 1].wait()
        for t in range(j * TOGETHER, (j + 1) * TOGETHER):
            first = f_ref[k, t, :, 0, :].astype(F32)
            last = f_ref[k, t, :, columns - 1, :].astype(F32)
            rows = pl.ds((k * tags + t) * levels, levels)
            inner_ref[rows, :] = jnp.where(even, last, first).astype(BF16)
            outer_ref[rows, :] = jnp.where(even, first, last).astype(BF16)


def staged(fractions, winds):
    species, tags, levels, _, lanes = fractions.shape
    whole = pl.BlockSpec(memory_space=pltpu.VMEM)
    far = pl.BlockSpec(memory_space=pltpu.HBM)
    rows = jax.ShapeDtypeStruct(((species * tags + 1) * levels, lanes), BF16)
    return pl.pallas_call(
        stage_kernel,
        out_shape=(
            jax.ShapeDtypeStruct(fractions.shape, fractions.dtype),
            jax.ShapeDtypeStruct(winds.shape, winds.dtype),
            rows,
            rows,
        ),
        in_specs=[far, far],
        out_specs=[whole] * 4,
        scratch_shapes=[pltpu.SemaphoreType.DMA((species * (tags // TOGETHER) + 1,))],
        compiler_params=LIMIT,
        name="stage",
    )(in_hbm(fractions), in_hbm(winds))


def tile_position():
    tile = lax.axis_index("tile")
    return tile == 0, tile == lax.axis_size("tile") - 1, tile % 2 == 0


def lower_half(low):
    inward = jnp.minimum(low, 0.0)
    return low - inward, inward


def upper_half(up):
    outward = jnp.maximum(up, 0.0)
    return outward - up, outward


def coefficients(cell_ext, wind_ext, winds_ref, flux_ext, coef):
    levels, columns, lanes = coef.shape[1:]
    lane = lax.broadcasted_iota(jnp.int32, (columns, lanes), 1)
    plane = [cell_ext[z, pl.ds(PAD, columns), :] for z in range(levels)]
    zero = jnp.zeros_like(plane[0])
    at = lambda z: plane[z] if 0 <= z < levels else zero
    flux_z = [zero]
    for z in range(1, levels):
        flux_z.append(winds_ref[2, z] * limited(at(z - 2), at(z - 1), at(z), at(z + 1)))
    flux_z.append(zero)
    for z in range(levels):
        flux_ext[z] = wind_ext[z] * limited(
            *(cell_ext[z, pl.ds(PAD - 2 + k, columns + 8), :] for k in range(4))
        )
        x_low = flux_ext[z, pl.ds(0, columns), :]
        x_up = flux_ext[z, pl.ds(1, columns), :]
        c = plane[z]
        y_two = jnp.where(lane < 2, 0.0, pltpu.roll(c, 2, 1))
        y_one = jnp.where(lane < 1, 0.0, pltpu.roll(c, 1, 1))
        y_next = jnp.where(lane == lanes - 1, 0.0, pltpu.roll(c, lanes - 1, 1))
        y_low = winds_ref[1, z] * limited(y_two, y_one, c, y_next)
        y_low = jnp.where(lane < 1, 0.0, y_low)
        y_up = pltpu.roll(y_low, lanes - 1, 1)
        centre = c
        for d, (low, up) in enumerate(((x_low, x_up), (y_low, y_up), (flux_z[z], flux_z[z + 1]))):
            coef[2 * d, z], inward = lower_half(low)
            coef[2 * d + 1, z], outward = upper_half(up)
            centre = centre + (inward - outward)
        coef[6, z] = centre


def stencil(coef, ext, sides, tag, count, put):
    levels, columns, lanes = coef.shape[1:]
    body = pl.ds(PAD, columns)
    planes = [[ext[tag + p, z, body, :] for z in range(levels)] for p in range(count)]
    for z in range(levels):
        cs = [coef[k, z] for k in range(7)]
        for p, plane in enumerate(planes):
            f = plane[z]
            total = cs[6] * f
            total += cs[0] * ext[tag + p, z, pl.ds(PAD - 1, columns), :]
            total += cs[1] * ext[tag + p, z, pl.ds(PAD + 1, columns), :]
            if sides is None:
                left, right = pltpu.roll(f, 1, 1), pltpu.roll(f, lanes - 1, 1)
            else:
                left, right = sides[0, tag + p, z], sides[1, tag + p, z]
            total += cs[2] * left
            total += cs[3] * right
            if z > 0:
                total += cs[4] * plane[z - 1]
            if z < levels - 1:
                total += cs[5] * plane[z + 1]
            put(tag + p, z, total)


def first_kernel(
    species_ref, cells_ref, winds_ref, inner_ref, outer_ref, f_ref, middle, partial, ext, sides,
    cell_ext, wind_ext, flux_ext, coef,
):
    _, tags, levels, columns, lanes = f_ref.shape
    own = species_ref[0]
    _, _, even = tile_position()
    blank = jnp.zeros((levels, PAD, lanes), F32)
    cell_ext[:, pl.ds(0, PAD), :] = blank
    cell_ext[:, pl.ds(PAD + columns, PAD), :] = blank
    for z in range(levels):
        cell_ext[z, pl.ds(PAD, columns), :] = decoded(cells_ref[pl.ds(z * columns, columns), :])
    row = lax.broadcasted_iota(jnp.int32, (levels, columns, lanes), 1)
    wind_ext[:, pl.ds(columns, 8), :] = blank
    wind_ext[:, pl.ds(0, columns), :] = jnp.where((row < 2) | (row == columns - 1), 0.0, winds_ref[0])
    coefficients(cell_ext, wind_ext, winds_ref, flux_ext, coef)

    def extend(k, i):
        which = own if k == 0 else 1 - own
        rows = pl.ds((which * tags + i) * levels, levels)
        from_inner, from_outer = inner_ref[rows, :].astype(F32), outer_ref[rows, :].astype(F32)
        ext[k, i, :, PAD - 1, :] = jnp.where(even, from_outer, from_inner)
        ext[k, i, :, PAD + columns, :] = jnp.where(even, from_inner, from_outer)
        for z in range(levels):
            ext[k, i, z, pl.ds(PAD, columns), :] = f_ref[which, i, z].astype(F32)

    def put(t, z, total):
        partial[t, z, 0] = total[:8]
        partial[t, z, 1] = total[columns - 8 :]
        middle[t, z] = total[8 : columns - 8].astype(middle.dtype)

    for j in range(0, tags, TOGETHER):
        for p in range(TOGETHER):
            extend(0, j + p)
        stencil(coef, ext.at[0], None, j, TOGETHER, put)
    for i in range(tags):
        extend(1, i)
        for z in range(levels):
            f = f_ref[1 - own, i, z].astype(F32)
            sides[0, i, z] = pltpu.roll(f, 1, 1)
            sides[1, i, z] = pltpu.roll(f, lanes - 1, 1)


def second_kernel(
    species_ref, cells_ref, own_ref, winds_ref, inner_ref, outer_ref, middle, partial, ext, sides, out_ref,
    cell_ext, wind_ext, flux_ext, coef, edge_wind, edge_coef, before, result, sems,
):
    _, tags, levels, padded, lanes = ext.shape
    columns = padded - 2 * PAD
    size = levels * columns
    mine = species_ref[0]
    first_tile, last_tile, even = tile_position()
    here = pl.ds(2 * tags * levels, levels)
    above = jnp.where(even, inner_ref[here, :].astype(F32), outer_ref[here, :].astype(F32))
    above = jnp.where(last_tile, 0.0, above)

    def load(source, k):
        def rim(row):
            kept = decoded(own_ref[pl.ds(size + (row + 2 * k) * levels, levels), :])
            return kept + decoded(cells_ref[pl.ds(size + (row + 2 - 2 * k) * levels, levels), :])

        for z in range(levels):
            cell_ext[z, pl.ds(PAD, columns), :] = decoded(source[pl.ds(z * columns, columns), :])
        for j in range(2):
            from_inner, from_outer = rim(j), rim(4 + j)
            low = jnp.where(even, from_outer, from_inner)
            high = jnp.where(even, from_inner, from_outer)
            cell_ext[:, PAD - 2 + j, :] = jnp.where(first_tile, 0.0, low)
            cell_ext[:, PAD + columns + j, :] = jnp.where(last_tile, 0.0, high)

    load(own_ref, 0)
    row = lax.broadcasted_iota(jnp.int32, (levels, 8, lanes), 1)
    blank = jnp.zeros((levels, 8, lanes), F32)
    open_low = (row == 1) | ((row == 0) & jnp.logical_not(first_tile))
    edge_wind[:, pl.ds(0, 8), :] = jnp.where(open_low, winds_ref[0, :, 0:8, :], 0.0)
    edge_wind[:, pl.ds(8, 8), :] = blank
    edge_wind[:, pl.ds(16, 8), :] = jnp.where(row == 7, winds_ref[0, :, columns - 8 :, :], 0.0)
    edge_wind[:, pl.ds(24, 8), :] = blank
    edge_wind[:, 24, :] = above
    starts = (PAD, PAD + columns - 8)
    for z in range(levels):
        for side, start in enumerate(starts):
            flux_ext[z, pl.ds(16 * side, 16), :] = edge_wind[z, pl.ds(16 * side, 16), :] * limited(
                *(cell_ext[z, pl.ds(start - 2 + k, 16), :] for k in range(4))
            )
            edge_coef[0, z, side], inward = lower_half(flux_ext[z, pl.ds(16 * side, 8), :])
            edge_coef[1, z, side], outward = upper_half(flux_ext[z, pl.ds(16 * side + 1, 8), :])
            edge_coef[2, z, side] = inward - outward
    for z in range(levels):
        cs = [[edge_coef[k, z, side] for k in range(3)] for side in range(2)]
        for t in range(tags):
            before[t, z, pl.ds(8, columns - 16), :] = middle[t, z]
            for side, start in enumerate(starts):
                total = partial[t, z, side] + cs[side][2] * ext[0, t, z, pl.ds(start, 8), :]
                total += cs[side][0] * ext[0, t, z, pl.ds(start - 1, 8), :]
                total += cs[side][1] * ext[0, t, z, pl.ds(start + 1, 8), :]
                before[t, z, pl.ds(start - PAD, 8), :] = total.astype(before.dtype)
    copies = [pltpu.make_async_copy(before, out_ref.at[1 - mine], sems.at[0])]
    copies[0].start()

    load(cells_ref, 1)
    wind_ext[:, pl.ds(0, columns), :] = winds_ref[0]
    wind_ext[:, 0, :] = jnp.where(first_tile, 0.0, winds_ref[0, :, 0, :])
    wind_ext[:, columns, :] = above
    coefficients(cell_ext, wind_ext, winds_ref, flux_ext, coef)

    def put(t, z, total):
        result[t, z] = total.astype(result.dtype)

    for j in range(0, tags, TOGETHER):
        stencil(coef, ext.at[1], sides, j, TOGETHER, put)
        part = pl.ds(j, TOGETHER)
        copies.append(pltpu.make_async_copy(result.at[part], out_ref.at[mine, part], sems.at[len(copies)]))
        copies[-1].start()
    for copy in copies:
        copy.wait()


def work_refs(levels, columns, lanes):
    return [
        pltpu.VMEM((levels, columns + 24, lanes), F32),
        pltpu.VMEM((levels, columns + 8, lanes), F32),
        pltpu.VMEM((levels, columns + 8, lanes), F32),
        pltpu.VMEM((7, levels, columns, lanes), F32),
    ]


def first_half(which, cells, winds, from_inner, from_outer, fractions):
    species, tags, levels, columns, lanes = fractions.shape
    whole = pl.BlockSpec(memory_space=pltpu.VMEM)
    return pl.pallas_call(
        first_kernel,
        out_shape=(
            jax.ShapeDtypeStruct((tags, levels, columns - 16, lanes), fractions.dtype),
            jax.ShapeDtypeStruct((tags, levels, 2, 8, lanes), F32),
            jax.ShapeDtypeStruct((species, tags, levels, columns + 2 * PAD, lanes), F32),
            jax.ShapeDtypeStruct((2, tags, levels, columns, lanes), F32),
        ),
        in_specs=[pl.BlockSpec(memory_space=pltpu.SMEM)] + [whole] * 5,
        out_specs=[whole] * 4,
        scratch_shapes=work_refs(levels, columns, lanes),
        compiler_params=LIMIT,
        name="first",
    )(which, in_vmem(cells), winds, in_vmem(from_inner), in_vmem(from_outer), fractions)


def second_half(which, cells, own, winds, from_inner, from_outer, middle, partial, ext, sides, like):
    _, tags, levels, columns, lanes = like.shape
    whole = pl.BlockSpec(memory_space=pltpu.VMEM)
    one = pltpu.VMEM((tags, levels, columns, lanes), like.dtype)
    return pl.pallas_call(
        second_kernel,
        out_shape=jax.ShapeDtypeStruct(like.shape, like.dtype),
        in_specs=[pl.BlockSpec(memory_space=pltpu.SMEM)] + [whole] * 9,
        out_specs=pl.BlockSpec(memory_space=pl.ANY),
        scratch_shapes=work_refs(levels, columns, lanes)
        + [
            pltpu.VMEM((levels, 32, lanes), F32),
            pltpu.VMEM((3, levels, 2, 8, lanes), F32),
            one,
            one,
            pltpu.SemaphoreType.DMA((tags // TOGETHER + 1,)),
        ],
        compiler_params=LIMIT,
        name="second",
    )(
        which, in_vmem(cells), in_vmem(own), winds, in_vmem(from_inner), in_vmem(from_outer),
        in_vmem(middle), in_vmem(partial), in_vmem(ext), in_vmem(sides),
    )


def shards(species_slot, bulk, winds, fractions):
    group, groups = lax.axis_index("tag"), lax.axis_size("tag")

    main, inner_edge, outer_edge = picked(species_slot, bulk)
    came = paired(main[1], "tag", inner)
    rim_outer = paired(outer_edge, "tile", outer)
    rim_inner = paired(inner_edge, "tile", inner)
    fractions, winds, inner_rows, outer_rows = staged(fractions, winds)
    own = jnp.concatenate([main[0] + came, rim_inner, rim_outer])
    bit = 2
    while bit < groups:
        came = paired(own, "tag", lambda i, count: i ^ bit)
        own = own + came
        bit *= 2
    got_inner = paired(inner_rows, "tile", inner)
    got_outer = paired(outer_rows, "tile", outer)
    other = paired(own, "tag", inner)
    which = lax.rem(group, 2)[None]
    half = first_half(which, own, winds, got_inner, got_outer, fractions)
    return second_half(1 - which, other, own, winds, got_inner, got_outer, *half, fractions)


def solution(mesh):
    placed = (
        P(),
        P("tag", None, "tile", None),
        P(None, None, "tile", None),
        P(None, "tag", None, "tile", None),
    )
    return jax.shard_map(
        shards,
        mesh=mesh,
        in_specs=placed,
        out_specs=P(None, "tag", None, "tile", None),
        check_vma=False,
    )
```
